32 devices in a mesh: groups: 2 (over y), seq: 4 (over z), chan: 2 (over x), sub: 2 (over core).
Axes of the slice: x: 2, y: 2, z: 4, core: 2. Of those that a mesh axis runs over, the one named last changes fastest.
Arguments:
- tokens: bfloat16 [16384, 2048], P(('groups', 'seq', 'sub'), 'chan'), parts along dimension 0, may hold values from -6 to 6
- low_angle: float32 [2048], P('chan'), may hold values from 0.1 to 1.47
- high_taps: float32 [2, 2048], P(None, 'chan'), may hold values from -3 to 3
- level_mix: float32 [17, 2048], P(None, 'chan'), may hold values from -1.5 to 1.5
- w_value: bfloat16 [2048, 2048], P(None, 'chan'), may hold values from -0.125 to 0.125
- w_gate: bfloat16 [2048, 2048], P(None, 'chan'), may hold values from -0.125 to 0.125
- out_weight: bfloat16 [2048, 2048], P(None, 'chan'), may hold values from -0.125 to 0.125
Outputs:
- result: bfloat16 [16384, 2048], P(('groups', 'seq', 'sub'), 'chan'), parts along dimension 0
The draws below stay inside these ranges and needn't reach their ends.
There are 2 independent parts, one for each index of `groups`. The reference program is written for one: setup_inputs(seed, part) draws one part's arguments, and reference() takes and returns one part's arrays. A program takes and returns all parts, laid end to end along the dimension named above; an argument that names none is the same for every part. Nothing has to cross between parts.
All inputs are finite; a program needn't handle non-finite values.
Results may differ from the reference program's by a relative error of at most 0.0043.
Values may be sent and summed in bfloat16 or wider, within the bound.
A program may use at most 128 MiB of HBM per device.

```python
import jax
import jax.numpy as jnp
from jax import lax

D = 2048
LEVELS = 15
TOKENS = 8192


def level_of(key, extent, cuts, least, top_value):
    gain = 1.0
    for axis_at, blocks in cuts:
        steps = jax.random.uniform(jax.random.fold_in(jax.random.fold_in(key, 6), axis_at), (blocks,), jnp.float32, least / len(cuts), top_value / len(cuts))
        gain = gain * jnp.repeat(jnp.exp(steps), extent[axis_at] // blocks).reshape((-1,) + (1,) * (len(extent) - 1 - axis_at))
    return gain


def noise(own_key, dims, scale, most, cuts=(), dtype=jnp.bfloat16):
    drawn = scale * jax.random.normal(own_key, dims, jnp.float32)
    if cuts:
        drawn = drawn * level_of(own_key, dims, cuts, -0.22, 0.18)
    return jnp.clip(drawn, -most, most).astype(dtype)


def setup_inputs(seed: int = 0, part: int = 0) -> dict:
    keys = jax.random.split(jax.random.key(seed), 8)
    part_splits = jax.random.split(jax.random.fold_in(keys[7], part), 8)
    return {
        "tokens": noise(part_splits[0], (TOKENS, D), 1.0, 6.0, ((0, 8), (1, 2))),
        "low_angle": jnp.clip(0.1 + 1.37 * jax.random.uniform(keys[1], (D,), jnp.float32) ** level_of(keys[1], (D,), ((0, 2),), -0.2, 0.2), 0.1, 1.47),
        "high_taps": noise(keys[2], (2, D), 0.7, 3.0, ((1, 2),), jnp.float32),
        "level_mix": noise(keys[3], (LEVELS + 2, D), (LEVELS + 2) ** -0.5, 1.5, ((1, 2),), jnp.float32),
        "w_value": noise(keys[4], (D, D), D ** -0.5, 0.125, ((1, 2),)),
        "w_gate": noise(keys[5], (D, D), D ** -0.5, 0.125, ((1, 2),)),
        "out_weight": noise(keys[6], (D, D), D ** -0.5, 0.125, ((1, 2),)),
    }


def filter_block(inputs):
    block, angle, high_pair, mix = inputs
    low0 = jnp.cos(angle)
    low1 = jnp.sin(angle)
    stream = block.astype(jnp.float32)
    length = stream.shape[0]
    mixed = mix[LEVELS + 1] * stream
    for level in range(LEVELS):
        reach = 2 ** level
        if reach < length:
            shifted = jnp.concatenate([jnp.zeros((reach, stream.shape[1]), jnp.float32), stream[:length - reach]], 0)
        else:
            shifted = jnp.zeros_like(stream)
        high = high_pair[0] * stream + high_pair[1] * shifted
        stream = low0 * stream + low1 * shifted
        mixed = mixed + mix[level] * high
    mixed = mixed + mix[LEVELS] * stream
    return jax.nn.gelu(mixed).astype(jnp.bfloat16)


def reference(tokens, low_angle, high_taps, level_mix, w_value, w_gate, out_weight):
    length = tokens.shape[0]
    width = tokens.shape[1]
    blocks = width // 256
    tok_blocks = tokens.reshape(length, blocks, 256).transpose(1, 0, 2)
    angle_blocks = low_angle.reshape(blocks, 256)
    high_blocks = high_taps.reshape(2, blocks, 256).transpose(1, 0, 2)
    mix_blocks = level_mix.reshape(LEVELS + 2, blocks, 256).transpose(1, 0, 2)
    activated = lax.map(filter_block, (tok_blocks, angle_blocks, high_blocks, mix_blocks))
    activated = activated.transpose(1, 0, 2).reshape(length, width)
    value = jnp.dot(activated, w_value, preferred_element_type=jnp.float32)
    gate = jnp.dot(activated, w_gate, preferred_element_type=jnp.float32)
    hidden = (value * jax.nn.sigmoid(gate)).astype(jnp.bfloat16)
    outcome = jnp.dot(hidden, out_weight, preferred_element_type=jnp.float32) + tokens.astype(jnp.float32)
    return outcome.astype(jnp.bfloat16)
```

```python
import functools

import jax
import jax.numpy as jnp
from jax import lax
from jax.experimental import pallas as pl
from jax.experimental.pallas import tpu as pltpu
from jax.sharding import PartitionSpec as P

MESH = pl.DeviceIdType.MESH
F32 = jnp.float32
BF16 = jnp.bfloat16
LANES = 128
STEP = 128
CHUNKS = 2
TILE = 256


def run_levels(stream, shifter, low0, low1, high0, high1, mix):
    levels = mix.shape[0] - 2
    mixed = mix[levels + 1] * stream
    for level in range(levels):
        shifted = shifter(stream, 2**level)
        high = high0 * stream + high1 * shifted
        stream = low0 * stream + low1 * shifted
        mixed = mixed + mix[level] * high
    return mixed + mix[levels] * stream


def plain(tokens, low_angle, high_taps, level_mix, w_value, w_gate, out_weight):
    rows = tokens.shape[0]
    channels = tokens.shape[1]
    ways = lax.axis_size(("seq", "sub"))
    total = rows * ways
    narrow = channels // ways
    place = lax.axis_index(("seq", "sub")) * narrow
    columns = lax.all_to_all(tokens.T, ("seq", "sub"), split_axis=0, concat_axis=1, tiled=True)
    angle = lax.dynamic_slice_in_dim(low_angle, place, narrow, 0)[:, None]
    high_pair = lax.dynamic_slice_in_dim(high_taps, place, narrow, 1)[:, :, None]
    mix = lax.dynamic_slice_in_dim(level_mix, place, narrow, 1)[:, :, None]

    def shifter(stream, reach):
        if reach >= total:
            return jnp.zeros_like(stream)
        return jnp.concatenate(
            [jnp.zeros((stream.shape[0], reach), F32), stream[:, : total - reach]], 1
        )

    mixed = run_levels(
        columns.astype(F32),
        shifter,
        jnp.cos(angle),
        jnp.sin(angle),
        high_pair[0],
        high_pair[1],
        mix,
    )
    filtered = jax.nn.gelu(mixed).astype(BF16)
    activated = lax.all_to_all(filtered, ("seq", "sub"), split_axis=1, concat_axis=0, tiled=True).T
    piece = lax.all_gather(activated, "chan", axis=1, tiled=True)
    value = jnp.dot(piece, w_value, preferred_element_type=F32)
    gate = jnp.dot(piece, w_gate, preferred_element_type=F32)
    hidden = (value * jax.nn.sigmoid(gate)).astype(BF16)
    projected = jnp.dot(
        lax.all_gather(hidden, "chan", axis=1, tiled=True),
        out_weight,
        preferred_element_type=F32,
    )
    return (projected + tokens.astype(F32)).astype(BF16)


def kernel(
    ways,
    tokens,
    trig,
    high_taps,
    level_mix,
    w_value,
    w_gate,
    out_weight,
    out,
    cols,
    hist,
    near,
    coef,
    act,
    piece,
    hid,
    wbuf,
    obuf,
    rbuf,
    own_sem,
    in_send,
    in_recv,
    wx_send,
    wx_recv,
    wy_send,
    wy_recv,
    wc_send,
    wc_recv,
    act_send,
    act_recv,
    local_sem,
    res_send,
    res_recv,
):
    rows, half = tokens.shape
    total = rows * ways
    levels = level_mix.shape[0] - 2
    subs = 2
    y = lax.axis_index("groups")
    z = lax.axis_index("seq")
    x = lax.axis_index("chan")
    u = lax.axis_index("sub")
    me = z * subs + u
    nx, ny, nu = 1 - x, 1 - y, 1 - u
    part = rows // 2
    chunk = part // CHUNKS
    quarter = wbuf.shape[2] // 4
    ws = (w_value, w_gate, out_weight)

    barrier = pltpu.get_barrier_semaphore()
    for other in range(1, 2 * ways):
        them = lax.rem(me * 2 + x + other, 2 * ways)
        pl.semaphore_signal(
            barrier,
            inc=1,
            device_id={"seq": them // 4, "sub": lax.rem(them // 2, 2), "chan": lax.rem(them, 2)},
            device_id_type=MESH,
        )
    pl.semaphore_signal(barrier, inc=1, device_id={"groups": ny}, device_id_type=MESH)
    pl.semaphore_wait(barrier, 2 * ways)

    def in_copy(peer, source):
        lanes = pl.ds(pl.multiple_of(peer * LANES, LANES), LANES)
        return pltpu.make_async_remote_copy(
            src_ref=tokens.at[:, lanes],
            dst_ref=cols.at[pl.ds(pl.multiple_of(source * rows, rows), rows)],
            send_sem=in_send.at[peer],
            recv_sem=in_recv.at[source],
            device_id={"seq": peer // subs, "sub": lax.rem(peer, subs)},
            device_id_type=MESH,
        )

    for other in range(1, ways):
        in_copy(lax.rem(me + other, ways), me).start()
    own_in = pltpu.make_async_copy(
        tokens.at[:, pl.ds(pl.multiple_of(me * LANES, LANES), LANES)],
        cols.at[pl.ds(pl.multiple_of(me * rows, rows), rows)],
        own_sem.at[3],
    )
    own_in.start()

    def band(index):
        return pl.ds(pl.multiple_of(index * quarter, quarter), quarter)

    mine, across = y * 2 + u, ny * 2 + u

    def x_copy(i):
        return pltpu.make_async_remote_copy(
            src_ref=ws[i].at[band(mine)],
            dst_ref=wbuf.at[i, x, band(mine)],
            send_sem=wx_send.at[i],
            recv_sem=wx_recv.at[i],
            device_id={"chan": nx},
            device_id_type=MESH,
        )

    def y_copy(i):
        return pltpu.make_async_remote_copy(
            src_ref=wbuf.at[i, nx, band(mine)],
            dst_ref=wbuf.at[i, nx, band(mine)],
            send_sem=wy_send.at[i],
            recv_sem=wy_recv.at[i],
            device_id={"groups": ny},
            device_id_type=MESH,
        )

    def c_copy(i, k):
        slot = wbuf.at[i, nx, band(mine if k == 0 else across)]
        return pltpu.make_async_remote_copy(
            src_ref=slot,
            dst_ref=slot,
            send_sem=wc_send.at[i, k],
            recv_sem=wc_recv.at[i, k],
            device_id={"sub": nu},
            device_id_type=MESH,
        )

    for i in range(3):
        x_copy(i).start()
    own_w = [pltpu.make_async_copy(ws[i], wbuf.at[i, x], own_sem.at[i]) for i in range(3)]
    for copy in own_w:
        copy.start()

    @pl.loop(0, total // STEP)
    def _(i):
        hist[pl.ds(pl.multiple_of(i * STEP, STEP), STEP)] = jnp.zeros((STEP, LANES), F32)

    near[...] = jnp.zeros_like(near)

    lanes = pl.ds(pl.multiple_of(me * LANES, LANES), LANES)
    low0, low1 = trig[0:1, lanes], trig[1:2, lanes]
    high0, high1 = high_taps[0:1, lanes], high_taps[1:2, lanes]
    mix = [level_mix[k : k + 1, lanes] for k in range(levels + 2)]
    slope = low0 / low1
    stay, step_up = high0 - high1 * slope, high1 / low1
    live = sum(2**k < total for k in range(levels))
    weights = [mix[levels + 1] + mix[0] * stay]
    scale = low0
    for k in range(1, levels + 1):
        weight = mix[k - 1] * step_up + (mix[k] * stay if k < levels else mix[k])
        weights.append(weight * scale)
        scale = scale * low0
    last = weights[live]
    for k in range(live + 1, levels + 1):
        last = last + weights[k]
    for k in range(live):
        coef[k : k + 1] = weights[k]
    coef[live : live + 1] = last
    coef[live + 1 : live + 2] = low1 / low0

    x_copy(0).wait_recv()
    y_copy(0).start()
    c_copy(0, 0).start()
    x_copy(1).wait_recv()
    y_copy(1).start()
    c_copy(1, 0).start()
    y_copy(0).wait_recv()
    c_copy(0, 1).start()

    def act_copy(owner, h, q, source, source_x):
        start = pl.multiple_of(owner * rows + h * part + q * chunk, chunk)
        to = pl.ds(pl.multiple_of(source_x * half + source * LANES, LANES), LANES)
        return pltpu.make_async_remote_copy(
            src_ref=act.at[pl.ds(start, chunk)],
            dst_ref=piece.at[q, :, to],
            send_sem=act_send.at[q, owner * 2 + h],
            recv_sem=act_recv.at[q, source * 2 + source_x],
            device_id={"seq": owner // subs, "sub": lax.rem(owner, subs), "chan": h},
            device_id_type=MESH,
        )

    def own_act(q):
        start = pl.multiple_of(me * rows + x * part + q * chunk, chunk)
        to = pl.ds(pl.multiple_of(x * half + me * LANES, LANES), LANES)
        return pltpu.make_async_copy(
            act.at[pl.ds(start, chunk)], piece.at[q, :, to], local_sem.at[q]
        )

    def send_act(owner, q):
        for h in range(2):
            mine_too = jnp.logical_and(owner == me, x == h)

            @pl.when(mine_too)
            def _():
                own_act(q).start()

            @pl.when(jnp.logical_not(mine_too))
            def _():
                act_copy(owner, h, q, me, x).start()

    def advance(at):
        s = cols[pl.ds(at, STEP)].astype(F32)
        tan = coef[live + 1 : live + 2]
        m = coef[0:1] * s
        for k in range(live):
            reach = 2**k
            if reach < 8:
                near[k, 8 : 8 + STEP] = s
                d = near[k, 8 - reach : 8 - reach + STEP]
                near[k, 0:8] = s[STEP - 8 :]
            elif reach < STEP:
                d = jnp.concatenate([hist[reach : 2 * reach], s[: STEP - reach]], 0)
                hist[reach : 2 * reach] = s[STEP - reach :]
            else:
                slot = pl.ds(pl.multiple_of(reach + lax.rem(at, reach), STEP), STEP)
                d = hist[slot]
                hist[slot] = s
            s = s + tan * d
            m = m + coef[k + 1 : k + 2] * s
        act[pl.ds(at, STEP)] = jax.nn.gelu(m).astype(BF16)

    own_in.wait()

    @pl.loop(0, ways)
    def _(block):
        @pl.when(block != me)
        def _():
            in_copy(block, block).wait_recv()

        @pl.loop(0, rows // STEP)
        def _(i):
            advance(pl.multiple_of(block * rows + i * STEP, STEP))

        @pl.when(block > 0)
        def _():
            send_act(block - 1, 0)

    send_act(ways - 1, 0)
    for q in range(1, CHUNKS):

        @pl.loop(0, ways)
        def _(owner):
            send_act(owner, q)

    y_copy(1).wait_recv()
    c_copy(1, 1).start()
    x_copy(2).wait_recv()
    y_copy(2).start()
    c_copy(2, 0).start()

    def weights_here(i):
        own_w[i].wait()
        for k in range(2):
            slot = wbuf.at[i, nx, band((y if k == 0 else ny) * 2 + nu)]
            pltpu.make_async_remote_copy(
                src_ref=slot,
                dst_ref=slot,
                send_sem=wc_send.at[i, k],
                recv_sem=wc_recv.at[i, k],
                device_id={"sub": nu},
                device_id_type=MESH,
            ).wait_recv()

    tiles = half // TILE

    def result_copy(q):
        return pltpu.make_async_remote_copy(
            src_ref=obuf.at[q],
            dst_ref=rbuf.at[q],
            send_sem=res_send.at[q],
            recv_sem=res_recv.at[q],
            device_id={"chan": nx},
            device_id_type=MESH,
        )

    for q in range(CHUNKS):
        own_act(q).wait()

        @pl.loop(1, 2 * ways)
        def _(other):
            them = lax.rem(me * 2 + x + other, 2 * ways)
            act_copy(me, x, q, them // 2, lax.rem(them, 2)).wait_recv()

        if q == 0:
            weights_here(0)
            weights_here(1)

        for h in range(2):

            @pl.loop(0, tiles)
            def _(tile):
                lanes = pl.ds(pl.multiple_of(tile * TILE, TILE), TILE)
                value = jnp.dot(piece[q], wbuf[0, h, :, lanes], preferred_element_type=F32)
                gate = jnp.dot(piece[q], wbuf[1, h, :, lanes], preferred_element_type=F32)
                to = pl.ds(pl.multiple_of(h * half + tile * TILE, TILE), TILE)
                hid[:, to] = (value * jax.nn.sigmoid(gate)).astype(BF16)

        if q == 0:
            y_copy(2).wait_recv()
            c_copy(2, 1).start()
            weights_here(2)

        @pl.loop(0, tiles)
        def _(tile):
            lanes = pl.ds(pl.multiple_of(tile * TILE, TILE), TILE)
            obuf[q, :, lanes] = jnp.dot(
                hid[...], wbuf[2, nx, :, lanes], preferred_element_type=F32
            ).astype(BF16)

        result_copy(q).start()
        at = pl.ds(pl.multiple_of(x * part + q * chunk, chunk), chunk)

        @pl.loop(0, tiles)
        def _(tile):
            lanes = pl.ds(pl.multiple_of(tile * TILE, TILE), TILE)
            projected = jnp.dot(hid[...], wbuf[2, x, :, lanes], preferred_element_type=F32)
            out[at, lanes] = (projected + tokens[at, lanes].astype(F32)).astype(BF16)

    for q in range(CHUNKS):
        result_copy(q).wait_recv()
        base = nx * part + q * chunk

        @pl.loop(0, chunk // 16)
        def _(i):
            at = pl.ds(pl.multiple_of(base + i * 16, 16), 16)
            got = rbuf[q, pl.ds(pl.multiple_of(i * 16, 16), 16)].astype(F32)
            out[at] = (got + tokens[at].astype(F32)).astype(BF16)

    @pl.loop(1, ways)
    def _(other):
        in_copy(lax.rem(me + other, ways), me).wait_send()

    for i in range(3):
        x_copy(i).wait_send()
        y_copy(i).wait_send()
        c_copy(i, 0).wait_send()
        c_copy(i, 1).wait_send()
    for q in range(CHUNKS):

        @pl.loop(1, 2 * ways)
        def _(other):
            them = lax.rem(me * 2 + x + other, 2 * ways)
            act_copy(them // 2, lax.rem(them, 2), q, me, x).wait_send()

        result_copy(q).wait_send()


def fused(tokens, low_angle, high_taps, level_mix, w_value, w_gate, out_weight):
    rows, half = tokens.shape
    depth = w_value.shape[0]
    ways = lax.axis_size(("seq", "sub"))
    total = rows * ways
    part = rows // 2
    chunk = part // CHUNKS
    trig = jnp.stack([jnp.cos(low_angle), jnp.sin(low_angle)])
    vmem = pl.BlockSpec(memory_space=pltpu.VMEM)
    hbm = pl.BlockSpec(memory_space=pl.ANY)
    dma = pltpu.SemaphoreType.DMA
    return pl.pallas_call(
        functools.partial(kernel, ways),
        out_shape=jax.ShapeDtypeStruct((rows, half), BF16),
        in_specs=[vmem, vmem, vmem, vmem, hbm, hbm, hbm],
        out_specs=vmem,
        scratch_shapes=[
            pltpu.VMEM((total, LANES), BF16),
            pltpu.VMEM((total, LANES), F32),
            pltpu.VMEM((3, STEP + 8, LANES), F32),
            pltpu.VMEM((level_mix.shape[0] + 7, LANES), F32),
            pltpu.VMEM((total, LANES), BF16),
            pltpu.VMEM((CHUNKS, chunk, depth), BF16),
            pltpu.VMEM((chunk, depth), BF16),
            pltpu.VMEM((3, 2, depth, half), BF16),
            pltpu.VMEM((CHUNKS, chunk, half), BF16),
            pltpu.VMEM((CHUNKS, chunk, half), BF16),
            dma((4,)),
            dma((ways,)),
            dma((ways,)),
            dma((3,)),
            dma((3,)),
            dma((3,)),
            dma((3,)),
            dma((3, 2)),
            dma((3, 2)),
            dma((CHUNKS, 2 * ways)),
            dma((CHUNKS, 2 * ways)),
            dma((CHUNKS,)),
            dma((CHUNKS,)),
            dma((CHUNKS,)),
        ],
        compiler_params=pltpu.CompilerParams(
            collective_id=0, has_side_effects=True, vmem_limit_bytes=60 * 1024 * 1024
        ),
        name="layer",
    )(tokens, trig, high_taps, level_mix, w_value, w_gate, out_weight)


def solution(mesh):
    pair = mesh.shape["groups"] == 2 and mesh.shape["chan"] == 2 and mesh.shape["sub"] == 2
    ways = mesh.shape["seq"] * mesh.shape["sub"]

    def shards(tokens, *rest):
        rows, half = tokens.shape
        fits = half == ways * LANES and rows % (2 * CHUNKS * STEP) == 0 and half % TILE == 0
        whole = rest[3].shape[0] == 2 * half and rows * ways * LANES <= 1 << 20
        body = fused if pair and fits and whole else plain
        return body(tokens, *rest)

    return jax.shard_map(
        shards,
        mesh=mesh,
        in_specs=(
            P(("groups", "seq", "sub"), "chan"),
            P("chan"),
            P(None, "chan"),
            P(None, "chan"),
            P(None, "chan"),
            P(None, "chan"),
            P(None, "chan"),
        ),
        out_specs=P(("groups", "seq", "sub"), "chan"),
        check_vma=False,
    )
```

```python
import functools

import jax
import jax.numpy as jnp
from jax import lax
from jax.experimental import pallas as pl
from jax.experimental.pallas import tpu as pltpu
from jax.sharding import PartitionSpec as P

MESH = pl.DeviceIdType.MESH
F32 = jnp.float32
BF16 = jnp.bfloat16
LANES = 128
STEP = 128
CHUNKS = 4
TILE = 512
PIECES = 4


def run_levels(stream, shifter, low0, low1, high0, high1, mix):
    levels = mix.shape[0] - 2
    mixed = mix[levels + 1] * stream
    for level in range(levels):
        shifted = shifter(stream, 2**level)
        high = high0 * stream + high1 * shifted
        stream = low0 * stream + low1 * shifted
        mixed = mixed + mix[level] * high
    return mixed + mix[levels] * stream


def plain(tokens, low_angle, high_taps, level_mix, w_value, w_gate, out_weight):
    rows = tokens.shape[0]
    channels = tokens.shape[1]
    ways = lax.axis_size(("seq", "sub"))
    total = rows * ways
    narrow = channels // ways
    place = lax.axis_index(("seq", "sub")) * narrow
    columns = lax.all_to_all(tokens.T, ("seq", "sub"), split_axis=0, concat_axis=1, tiled=True)
    angle = lax.dynamic_slice_in_dim(low_angle, place, narrow, 0)[:, None]
    high_pair = lax.dynamic_slice_in_dim(high_taps, place, narrow, 1)[:, :, None]
    mix = lax.dynamic_slice_in_dim(level_mix, place, narrow, 1)[:, :, None]

    def shifter(stream, reach):
        if reach >= total:
            return jnp.zeros_like(stream)
        return jnp.concatenate(
            [jnp.zeros((stream.shape[0], reach), F32), stream[:, : total - reach]], 1
        )

    mixed = run_levels(
        columns.astype(F32),
        shifter,
        jnp.cos(angle),
        jnp.sin(angle),
        high_pair[0],
        high_pair[1],
        mix,
    )
    filtered = jax.nn.gelu(mixed).astype(BF16)
    activated = lax.all_to_all(filtered, ("seq", "sub"), split_axis=1, concat_axis=0, tiled=True).T
    piece = lax.all_gather(activated, "chan", axis=1, tiled=True)
    value = jnp.dot(piece, w_value, preferred_element_type=F32)
    gate = jnp.dot(piece, w_gate, preferred_element_type=F32)
    hidden = (value * jax.nn.sigmoid(gate)).astype(BF16)
    projected = jnp.dot(
        lax.all_gather(hidden, "chan", axis=1, tiled=True),
        out_weight,
        preferred_element_type=F32,
    )
    return (projected + tokens.astype(F32)).astype(BF16)


def kernel(
    ways,
    tokens,
    trig,
    high_taps,
    level_mix,
    w_value,
    w_gate,
    out_weight,
    out,
    cols,
    hist,
    near,
    coef,
    act,
    piece,
    hid,
    wbuf,
    obuf,
    rbuf,
    own_sem,
    in_send,
    in_recv,
    wx_send,
    wx_recv,
    wy_send,
    wy_recv,
    wc_send,
    wc_recv,
    act_send,
    act_recv,
    local_sem,
    res_send,
    res_recv,
):
    rows, half = tokens.shape
    total = rows * ways
    levels = level_mix.shape[0] - 2
    subs = 2
    y = lax.axis_index("groups")
    z = lax.axis_index("seq")
    x = lax.axis_index("chan")
    u = lax.axis_index("sub")
    me = z * subs + u
    nx, ny, nu = 1 - x, 1 - y, 1 - u
    part = rows // 2
    chunk = part // CHUNKS
    quarter = wbuf.shape[2] // 4
    ws = (w_value, w_gate, out_weight)

    barrier = pltpu.get_barrier_semaphore()
    for other in range(1, 2 * ways):
        them = lax.rem(me * 2 + x + other, 2 * ways)
        pl.semaphore_signal(
            barrier,
            inc=1,
            device_id={"seq": them // 4, "sub": lax.rem(them // 2, 2), "chan": lax.rem(them, 2)},
            device_id_type=MESH,
        )
    pl.semaphore_signal(barrier, inc=1, device_id={"groups": ny}, device_id_type=MESH)
    pl.semaphore_wait(barrier, 2 * ways)

    def in_copy(peer, source):
        lanes = pl.ds(pl.multiple_of(peer * LANES, LANES), LANES)
        return pltpu.make_async_remote_copy(
            src_ref=tokens.at[:, lanes],
            dst_ref=cols.at[pl.ds(pl.multiple_of(source * rows, rows), rows)],
            send_sem=in_send.at[peer],
            recv_sem=in_recv.at[source],
            device_id={"seq": peer // subs, "sub": lax.rem(peer, subs)},
            device_id_type=MESH,
        )

    for other in range(1, ways):
        in_copy(lax.rem(me + other, ways), me).start()
    own_in = pltpu.make_async_copy(
        tokens.at[:, pl.ds(pl.multiple_of(me * LANES, LANES), LANES)],
        cols.at[pl.ds(pl.multiple_of(me * rows, rows), rows)],
        own_sem.at[3],
    )
    own_in.start()

    def band(index, k):
        fine = quarter // PIECES
        return pl.ds(pl.multiple_of(index * quarter + k * fine, fine), fine)

    mine, across = y * 2 + u, ny * 2 + u

    def x_copy(p):
        i, k = divmod(p, PIECES)
        return pltpu.make_async_remote_copy(
            src_ref=ws[i].at[band(mine, k)],
            dst_ref=wbuf.at[i, x, band(mine, k)],
            send_sem=wx_send.at[p],
            recv_sem=wx_recv.at[p],
            device_id={"chan": nx},
            device_id_type=MESH,
        )

    def y_copy(p):
        i, k = divmod(p, PIECES)
        return pltpu.make_async_remote_copy(
            src_ref=wbuf.at[i, nx, band(mine, k)],
            dst_ref=wbuf.at[i, nx, band(mine, k)],
            send_sem=wy_send.at[p],
            recv_sem=wy_recv.at[p],
            device_id={"groups": ny},
            device_id_type=MESH,
        )

    def c_copy(p, side, index):
        i, k = divmod(p, PIECES)
        slot = wbuf.at[i, nx, band(index, k)]
        return pltpu.make_async_remote_copy(
            src_ref=slot,
            dst_ref=slot,
            send_sem=wc_send.at[p, side],
            recv_sem=wc_recv.at[p, side],
            device_id={"sub": nu},
            device_id_type=MESH,
        )

    def relay_y(p):
        y_copy(p).wait_recv()
        c_copy(p, 1, across).start()

    def relay(p):
        x_copy(p).wait_recv()
        y_copy(p).start()
        c_copy(p, 0, mine).start()
        if p > 0:
            relay_y(p - 1)

    count = 3 * PIECES
    late = 10 * count // 12
    for p in range(late):
        x_copy(p).start()
    own_w = [pltpu.make_async_copy(ws[i], wbuf.at[i, x], own_sem.at[i]) for i in range(3)]
    for copy in own_w:
        copy.start()

    @pl.loop(0, total // STEP)
    def _(i):
        hist[pl.ds(pl.multiple_of(i * STEP, STEP), STEP)] = jnp.zeros((STEP, LANES), F32)

    near[...] = jnp.zeros_like(near)

    lanes = pl.ds(pl.multiple_of(me * LANES, LANES), LANES)
    low0, low1 = trig[0:1, lanes], trig[1:2, lanes]
    high0, high1 = high_taps[0:1, lanes], high_taps[1:2, lanes]
    mix = [level_mix[k : k + 1, lanes] for k in range(levels + 2)]
    slope = low0 / low1
    stay, step_up = high0 - high1 * slope, high1 / low1
    live = sum(2**k < total for k in range(levels))
    weights = [mix[levels + 1] + mix[0] * stay]
    scale = low0
    for k in range(1, levels + 1):
        weight = mix[k - 1] * step_up + (mix[k] * stay if k < levels else mix[k])
        weights.append(weight * scale)
        scale = scale * low0
    last = weights[live]
    for k in range(live + 1, levels + 1):
        last = last + weights[k]
    for k in range(live):
        coef[k : k + 1] = weights[k]
    coef[live : live + 1] = last
    coef[live + 1 : live + 2] = low1 / low0

    early = 7 * count // 12
    for p in range(early):
        relay(p)

    def act_copy(owner, h, q, source, source_x):
        start = pl.multiple_of(owner * rows + h * part + q * chunk, chunk)
        to = pl.ds(pl.multiple_of(source_x * half + source * LANES, LANES), LANES)
        return pltpu.make_async_remote_copy(
            src_ref=act.at[pl.ds(start, chunk)],
            dst_ref=piece.at[q, :, to],
            send_sem=act_send.at[q, owner * 2 + h],
            recv_sem=act_recv.at[q, source * 2 + source_x],
            device_id={"seq": owner // subs, "sub": lax.rem(owner, subs), "chan": h},
            device_id_type=MESH,
        )

    def own_act(q):
        start = pl.multiple_of(me * rows + x * part + q * chunk, chunk)
        to = pl.ds(pl.multiple_of(x * half + me * LANES, LANES), LANES)
        return pltpu.make_async_copy(
            act.at[pl.ds(start, chunk)], piece.at[q, :, to], local_sem.at[q]
        )

    def send_act(owner, q):
        for h in range(2):
            mine_too = jnp.logical_and(owner == me, x == h)

            @pl.when(mine_too)
            def _():
                own_act(q).start()

            @pl.when(jnp.logical_not(mine_too))
            def _():
                act_copy(owner, h, q, me, x).start()

    def advance(at):
        s = cols[pl.ds(at, STEP)].astype(F32)
        tan = coef[live + 1 : live + 2]
        m = coef[0:1] * s
        for k in range(live):
            reach = 2**k
            if reach < 8:
                near[k, 8 : 8 + STEP] = s
                d = near[k, 8 - reach : 8 - reach + STEP]
                near[k, 0:8] = s[STEP - 8 :]
            elif reach < STEP:
                d = jnp.concatenate([hist[reach : 2 * reach], s[: STEP - reach]], 0)
                hist[reach : 2 * reach] = s[STEP - reach :]
            else:
                slot = pl.ds(pl.multiple_of(reach + lax.rem(at, reach), STEP), STEP)
                d = hist[slot]
                hist[slot] = s
            s = s + tan * d
            m = m + coef[k + 1 : k + 2] * s
        act[pl.ds(at, STEP)] = jax.nn.gelu(m).astype(BF16)

    own_in.wait()

    @pl.loop(0, ways)
    def _(block):
        @pl.when(block != me)
        def _():
            in_copy(block, block).wait_recv()

        @pl.loop(0, rows // STEP)
        def _(i):
            advance(pl.multiple_of(block * rows + i * STEP, STEP))

        @pl.when(block > 0)
        def _():
            send_act(block - 1, 0)

        for p in range(early, late):

            @pl.when(block == 1 + (p - early) * 5 // 2)
            def _():
                relay(p)

    send_act(ways - 1, 0)
    for p in range(late, count):
        x_copy(p).start()
    for q in range(1, CHUNKS):

        @pl.loop(0, ways)
        def _(owner):
            send_act(owner, q)

    def weights_here(i):
        own_w[i].wait()
        for p in range(i * PIECES, (i + 1) * PIECES):
            c_copy(p, 0, y * 2 + nu).wait_recv()
            c_copy(p, 1, ny * 2 + nu).wait_recv()

    tiles = half // TILE

    def result_copy(q):
        return pltpu.make_async_remote_copy(
            src_ref=obuf.at[q],
            dst_ref=rbuf.at[q],
            send_sem=res_send.at[q],
            recv_sem=res_recv.at[q],
            device_id={"chan": nx},
            device_id_type=MESH,
        )

    def widen(q):
        own_act(q).wait()

        @pl.loop(1, 2 * ways)
        def _(other):
            them = lax.rem(me * 2 + x + other, 2 * ways)
            act_copy(me, x, q, them // 2, lax.rem(them, 2)).wait_recv()

        if q == 0:
            weights_here(0)
            weights_here(1)

        for h in range(2):

            @pl.loop(0, tiles)
            def _(tile):
                lanes = pl.ds(pl.multiple_of(tile * TILE, TILE), TILE)
                value = jnp.dot(piece[q], wbuf[0, h, :, lanes], preferred_element_type=F32)
                gate = jnp.dot(piece[q], wbuf[1, h, :, lanes], preferred_element_type=F32)
                to = pl.ds(pl.multiple_of(h * half + tile * TILE, TILE), TILE)
                hid[q % 2, :, to] = (value * jax.nn.sigmoid(gate)).astype(BF16)

    def project(q):
        @pl.loop(0, tiles)
        def _(tile):
            lanes = pl.ds(pl.multiple_of(tile * TILE, TILE), TILE)
            obuf[q, :, lanes] = jnp.dot(
                hid[q % 2], wbuf[2, nx, :, lanes], preferred_element_type=F32
            ).astype(BF16)

        result_copy(q).start()
        at = pl.ds(pl.multiple_of(x * part + q * chunk, chunk), chunk)

        @pl.loop(0, tiles)
        def _(tile):
            lanes = pl.ds(pl.multiple_of(tile * TILE, TILE), TILE)
            projected = jnp.dot(hid[q % 2], wbuf[2, x, :, lanes], preferred_element_type=F32)
            out[at, lanes] = (projected + tokens[at, lanes].astype(F32)).astype(BF16)

    widen(0)
    for p in range(late, count):
        relay(p)
    widen(1)
    relay_y(count - 1)
    weights_here(2)
    project(0)
    project(1)
    for q in range(2, CHUNKS):
        widen(q)
        project(q)

    for q in range(CHUNKS):
        result_copy(q).wait_recv()
        base = nx * part + q * chunk

        @pl.loop(0, chunk // 16)
        def _(i):
            at = pl.ds(pl.multiple_of(base + i * 16, 16), 16)
            got = rbuf[q, pl.ds(pl.multiple_of(i * 16, 16), 16)].astype(F32)
            out[at] = (got + tokens[at].astype(F32)).astype(BF16)

    @pl.loop(1, ways)
    def _(other):
        in_copy(lax.rem(me + other, ways), me).wait_send()

    for p in range(count):
        x_copy(p).wait_send()
        y_copy(p).wait_send()
        c_copy(p, 0, mine).wait_send()
        c_copy(p, 1, across).wait_send()
    for q in range(CHUNKS):

        @pl.loop(1, 2 * ways)
        def _(other):
            them = lax.rem(me * 2 + x + other, 2 * ways)
            act_copy(them // 2, lax.rem(them, 2), q, me, x).wait_send()

        result_copy(q).wait_send()


def fused(tokens, low_angle, high_taps, level_mix, w_value, w_gate, out_weight):
    rows, half = tokens.shape
    depth = w_value.shape[0]
    ways = lax.axis_size(("seq", "sub"))
    total = rows * ways
    part = rows // 2
    chunk = part // CHUNKS
    trig = jnp.stack([jnp.cos(low_angle), jnp.sin(low_angle)])
    vmem = pl.BlockSpec(memory_space=pltpu.VMEM)
    hbm = pl.BlockSpec(memory_space=pl.ANY)
    dma = pltpu.SemaphoreType.DMA
    return pl.pallas_call(
        functools.partial(kernel, ways),
        out_shape=jax.ShapeDtypeStruct((rows, half), BF16),
        in_specs=[vmem, vmem, vmem, vmem, hbm, hbm, hbm],
        out_specs=vmem,
        scratch_shapes=[
            pltpu.VMEM((total, LANES), BF16),
            pltpu.VMEM((total, LANES), F32),
            pltpu.VMEM((3, STEP + 8, LANES), F32),
            pltpu.VMEM((level_mix.shape[0] + 7, LANES), F32),
            pltpu.VMEM((total, LANES), BF16),
            pltpu.VMEM((CHUNKS, chunk, depth), BF16),
            pltpu.VMEM((2, chunk, depth), BF16),
            pltpu.VMEM((3, 2, depth, half), BF16),
            pltpu.VMEM((CHUNKS, chunk, half), BF16),
            pltpu.VMEM((CHUNKS, chunk, half), BF16),
            dma((4,)),
            dma((ways,)),
            dma((ways,)),
            dma((3 * PIECES,)),
            dma((3 * PIECES,)),
            dma((3 * PIECES,)),
            dma((3 * PIECES,)),
            dma((3 * PIECES, 2)),
            dma((3 * PIECES, 2)),
            dma((CHUNKS, 2 * ways)),
            dma((CHUNKS, 2 * ways)),
            dma((CHUNKS,)),
            dma((CHUNKS,)),
            dma((CHUNKS,)),
        ],
        compiler_params=pltpu.CompilerParams(
            collective_id=0, has_side_effects=True, vmem_limit_bytes=60 * 1024 * 1024
        ),
        name="layer",
    )(tokens, trig, high_taps, level_mix, w_value, w_gate, out_weight)


def solution(mesh):
    pair = mesh.shape["groups"] == 2 and mesh.shape["chan"] == 2 and mesh.shape["sub"] == 2
    ways = mesh.shape["seq"] * mesh.shape["sub"]

    def shards(tokens, *rest):
        rows, half = tokens.shape
        fits = half == ways * LANES and rows % STEP == 0 and rows % (32 * CHUNKS) == 0 and half % TILE == 0
        whole = rest[3].shape[0] == 2 * half and rows * ways * LANES <= 1 << 20
        body = fused if pair and fits and whole else plain
        return body(tokens, *rest)

    return jax.shard_map(
        shards,
        mesh=mesh,
        in_specs=(
            P(("groups", "seq", "sub"), "chan"),
            P("chan"),
            P(None, "chan"),
            P(None, "chan"),
            P(None, "chan"),
            P(None, "chan"),
            P(None, "chan"),
        ),
        out_specs=P(("groups", "seq", "sub"), "chan"),
        check_vma=False,
    )
```
